32 devices in a mesh: dp: 8 (over y, x, core), tensor: 4 (over z).
Axes of the slice: x: 2, y: 2, z: 4, core: 2. Of those that a mesh axis runs over, the one named last changes fastest.
Arguments:
- hidden_in: bfloat16 [16384, 768], P('dp'), may hold values from -6 to 6
- query_weight: bfloat16 [768, 768], P(None, 'tensor'), may hold values from -0.21875 to 0.21875
- query_bias: bfloat16 [768], P('tensor'), may hold values from -3 to 3
- key_weight: bfloat16 [768, 768], P(None, 'tensor'), may hold values from -0.21875 to 0.21875
- value_weight: bfloat16 [768, 768], P(None, 'tensor'), may hold values from -0.21875 to 0.21875
- value_bias: bfloat16 [768], P('tensor'), may hold values from -3 to 3
- output_weight: bfloat16 [768, 768], P('tensor'), may hold values from -2.5 to 2.5
- output_bias: bfloat16 [768], replicated, may hold values from -3 to 3
- attn_gain: bfloat16 [768], replicated, may hold values from 0.25 to 1.75
- attn_shift: bfloat16 [768], replicated, may hold values from -3 to 3
- up_weight: bfloat16 [768, 3072], P(None, 'tensor'), may hold values from -0.21875 to 0.21875
- up_bias: bfloat16 [3072], P('tensor'), may hold values from -3 to 3
- down_weight: bfloat16 [3072, 768], P('tensor'), may hold values from -0.109375 to 0.109375
- down_bias: bfloat16 [768], replicated, may hold values from -3 to 3
- ffn_gain: bfloat16 [768], replicated, may hold values from 0.25 to 1.75
- ffn_shift: bfloat16 [768], replicated, may hold values from -3 to 3
- cotangent: bfloat16 [16384, 768], P('dp'), may hold values from -6 to 6
Outputs:
- layer_out: bfloat16 [16384, 768], P('dp')
- input_grad: bfloat16 [16384, 768], P('dp')
- query_weight_grad: float32 [768, 768], P(None, 'tensor')
- query_bias_grad: float32 [768], P('tensor')
- key_weight_grad: float32 [768, 768], P(None, 'tensor')
- value_weight_grad: float32 [768, 768], P(None, 'tensor')
- value_bias_grad: float32 [768], P('tensor')
- output_weight_grad: float32 [768, 768], P('tensor')
- output_bias_grad: float32 [768], replicated
- attn_gain_grad: float32 [768], replicated
- attn_shift_grad: float32 [768], replicated
- up_weight_grad: float32 [768, 3072], P(None, 'tensor')
- up_bias_grad: float32 [3072], P('tensor')
- down_weight_grad: float32 [3072, 768], P('tensor')
- down_bias_grad: float32 [768], replicated
- ffn_gain_grad: float32 [768], replicated
- ffn_shift_grad: float32 [768], replicated
The draws below stay inside these ranges and needn't reach their ends.
All inputs are finite; a program needn't handle non-finite values.
Results may differ from the reference program's by a relative error of at most 0.023.
Values may be sent and summed in bfloat16 or wider, within the bound.
No kernel may reach another device: no remote copies, remote signals or barrier semaphores. Data moves between devices by JAX's collectives and lax.ppermute only.
A program may use at most 192 MiB of HBM per device.

```python
import jax
import jax.numpy as jnp
from jax import lax

D = 768
HEADS = 12
FF = 3072
LEN = 512
SEQ_DEV = 4
HDIM = 64
TOKENS = 16384
N_DP = 8
N_TENSOR = 4


def levels(own_key, extent, shards, smallest, high):
    level, own = 1.0, jax.random.fold_in(own_key, 6)
    for position, shards_of in shards:
        heights = jnp.exp(jax.random.uniform(jax.random.fold_in(own, position), (shards_of,), jnp.float32, smallest / len(shards), high / len(shards)))
        level = level * jnp.repeat(heights, extent[position] // shards_of).reshape([-1 if axis == position else 1 for axis in range(len(extent))])
    return level


def normal_values(rng, extent, scale, most, cuts=(), kind=jnp.bfloat16):
    factor_of = levels(rng, extent, cuts, -0.22, 0.18) if cuts else 1.0
    array = jax.random.normal(rng, extent, jnp.float32) * scale * factor_of
    return jnp.minimum(jnp.maximum(array, -most), most).astype(kind)


def setup_inputs(seed: int = 0) -> dict:
    keys = jax.random.split(jax.random.key(seed), 18)
    hidden_in = normal_values(keys[0], (TOKENS, D), 1.0, 6.0, ((0, 8),))
    query_weight = normal_values(keys[1], (D, D), D ** -0.5, 0.21875, ((1, 4),))
    query_bias = normal_values(keys[2], (D,), 0.5, 3.0, ((0, 4),))
    key_weight = normal_values(keys[3], (D, D), D ** -0.5, 0.21875, ((1, 4),))
    value_weight = normal_values(keys[4], (D, D), D ** -0.5, 0.21875, ((1, 4),))
    value_bias = normal_values(keys[5], (D,), 0.5, 3.0, ((0, 4),))
    output_weight = normal_values(keys[6], (D, D), (D * 4 // LEN) ** -0.5, 2.5, ((0, 4),))
    output_bias = normal_values(keys[7], (D,), 0.5, 3.0)
    attn_gain = jnp.clip(1.0 + 0.15 * jax.random.normal(keys[8], (D,), jnp.float32), 0.25, 1.75).astype(jnp.bfloat16)
    attn_shift = normal_values(keys[9], (D,), 0.5, 3.0)
    up_weight = normal_values(keys[10], (D, FF), D ** -0.5, 0.21875, ((1, 4),))
    up_bias = normal_values(keys[11], (FF,), 0.5, 3.0, ((0, 4),))
    down_weight = normal_values(keys[12], (FF, D), FF ** -0.5, 0.109375, ((0, 4),))
    down_bias = normal_values(keys[13], (D,), 0.5, 3.0)
    ffn_gain = jnp.clip(1.0 + 0.15 * jax.random.normal(keys[14], (D,), jnp.float32), 0.25, 1.75).astype(jnp.bfloat16)
    ffn_shift = normal_values(keys[15], (D,), 0.5, 3.0)
    cotangent = normal_values(keys[16], (TOKENS, D), 1.0, 6.0, ((0, 8),))
    return dict(hidden_in=hidden_in, query_weight=query_weight, query_bias=query_bias, key_weight=key_weight, value_weight=value_weight, value_bias=value_bias, output_weight=output_weight, output_bias=output_bias, attn_gain=attn_gain, attn_shift=attn_shift, up_weight=up_weight, up_bias=up_bias, down_weight=down_weight, down_bias=down_bias, ffn_gain=ffn_gain, ffn_shift=ffn_shift, cotangent=cotangent)


epsilon = 1e-12
highest = lax.Precision.HIGHEST

@jax.custom_vjp
def low(v):
    return lax.optimization_barrier(v.astype(jnp.bfloat16)).astype(jnp.float32)

@jax.custom_vjp
def low_back(v):
    return v

def low_keep(v):
    return (low(v), None)

def low_pass(kept, grad):
    return (grad,)

def back_keep(v):
    return (v, None)

def back_low(kept, grad):
    return (low(grad),)
low.defvjp(low_keep, low_pass)
low_back.defvjp(back_keep, back_low)

def matmul(left, right):
    return jnp.dot(left, right, precision=highest)

def layer_norm(values, norm_gain, norm_shift):
    center = values - lax.optimization_barrier(jnp.mean(values, axis=-1, keepdims=True))
    spread = lax.optimization_barrier(jnp.mean(center * center, axis=-1, keepdims=True))
    return center * lax.rsqrt(spread + epsilon) * norm_gain + norm_shift

def forward(params, inputs):
    query_weight, query_bias, key_weight, value_weight, value_bias, output_weight, output_bias, attn_gain, attn_shift, up_weight, up_bias, down_weight, down_bias, ffn_gain, ffn_shift = params
    row_count = inputs.shape[0]
    seq_count = row_count // LEN
    group_width = D // N_TENSOR
    group_heads = HEADS // N_TENSOR
    group_hidden = FF // N_TENSOR
    score_scale = HDIM ** (-0.5)
    head_shape = (seq_count, LEN, group_heads, HDIM)
    attn_total = jnp.zeros((row_count, D), jnp.float32)
    for group_index in range(N_TENSOR):
        col_slice = slice(group_index * group_width, (group_index + 1) * group_width)
        source = low_back(inputs)
        queries = low_back(low(matmul(source, query_weight[:, col_slice]) + query_bias[col_slice]))
        key_rows = low_back(low(matmul(source, key_weight[:, col_slice])))
        value_rows = low_back(low(matmul(source, value_weight[:, col_slice]) + value_bias[col_slice]))
        scores = jnp.einsum('bqhd,bkhd->bhqk', queries.reshape(head_shape), key_rows.reshape(head_shape), precision=highest) * score_scale
        scores = low_back(scores)
        attn_probs = low(jax.nn.softmax(scores, axis=-1))
        mixed_rows = jnp.einsum('bhqk,bkhd->bqhd', attn_probs, value_rows.reshape(head_shape), precision=highest)
        mixed_rows = low_back(low(mixed_rows.reshape(row_count, group_width)))
        attn_total = attn_total + low(matmul(mixed_rows, output_weight[col_slice, :]))
    attn_total = low_back(attn_total)
    normed = layer_norm(inputs + attn_total + output_bias, attn_gain, attn_shift)
    ffn_source = low(normed)
    ffn_total = jnp.zeros((row_count, D), jnp.float32)
    for group_index in range(N_TENSOR):
        hidden_slice = slice(group_index * group_hidden, (group_index + 1) * group_hidden)
        source = low_back(ffn_source)
        pre_act = low_back(matmul(source, up_weight[:, hidden_slice]) + up_bias[hidden_slice])
        active = low_back(low(jax.nn.gelu(pre_act, approximate=False)))
        ffn_total = ffn_total + low(matmul(active, down_weight[hidden_slice, :]))
    ffn_total = low_back(ffn_total)
    return layer_norm(normed + ffn_total + down_bias, ffn_gain, ffn_shift)

def reference(hidden_in, query_weight, query_bias, key_weight, value_weight, value_bias, output_weight, output_bias, attn_gain, attn_shift, up_weight, up_bias, down_weight, down_bias, ffn_gain, ffn_shift, cotangent):
    params = tuple((item.astype(jnp.float32) for item in (query_weight, query_bias, key_weight, value_weight, value_bias, output_weight, output_bias, attn_gain, attn_shift, up_weight, up_bias, down_weight, down_bias, ffn_gain, ffn_shift)))
    blocks = hidden_in.astype(jnp.float32).reshape(N_DP, SEQ_DEV * LEN, D)
    cot_blocks = cotangent.astype(jnp.float32).reshape(N_DP, SEQ_DEV * LEN, D)

    def block_step(totals, block_pair):
        block_in, block_cot = block_pair
        result, pullback = jax.vjp(forward, params, block_in)
        grads_params, grad_block = pullback(block_cot)
        totals = jax.tree.map(jnp.add, totals, grads_params)
        return (totals, (result.astype(jnp.bfloat16), grad_block.astype(jnp.bfloat16)))
    initial = tuple((jnp.zeros_like(item) for item in params))
    totals, (results, grad_rows) = lax.scan(block_step, initial, (blocks, cot_blocks))
    return (results.reshape(TOKENS, D), grad_rows.reshape(TOKENS, D), totals[0], totals[1], totals[2], totals[3], totals[4], totals[5], totals[6], totals[7], totals[8], totals[9], totals[10], totals[11], totals[12], totals[13], totals[14])
```

```python
import jax
import jax.numpy as jnp
from jax import lax
from jax.sharding import PartitionSpec as P

LEN = 512
HDIM = 64
GROUP = 8
epsilon = 1e-12
root_half = 0.7071067811865476
density_norm = 0.3989422804014327
f32 = jnp.float32
bf16 = jnp.bfloat16


def norm_parts(values):
    center = values - jnp.mean(values, axis=-1, keepdims=True)
    inverse = lax.rsqrt(jnp.mean(center * center, axis=-1, keepdims=True) + epsilon)
    return center * inverse, inverse


def norm_back(grad_out, normal, inverse, norm_gain):
    scaled = grad_out * norm_gain.astype(f32)
    first_mean = jnp.mean(scaled, axis=-1, keepdims=True)
    cross_mean = jnp.mean(scaled * normal, axis=-1, keepdims=True)
    return inverse * (scaled - first_mean - normal * cross_mean)


def dot(left, right, dims):
    return lax.dot_general(left, right, (dims, ((), ())), preferred_element_type=f32)


def gelu_slope(values):
    return (
        0.5 * (1.0 + lax.erf(values * root_half))
        + values * jnp.exp(-0.5 * values * values) * density_norm
    )


def make_shards(n_dp, n_tensor):
    def flip_dp(values, bit):
        return lax.ppermute(values, "dp", [(i, i ^ bit) for i in range(n_dp)])

    def flip_core(values):
        return flip_dp(values, 1)

    def flip_x(values):
        return flip_dp(values, 2)

    def flip_y(values):
        return flip_dp(values, 4)

    def flip_tensor(values, bit):
        return lax.ppermute(values, "tensor", [(i, i ^ bit) for i in range(n_tensor)])

    def ring(values):
        return lax.ppermute(values, "tensor", [(i, (i + 1) % n_tensor) for i in range(n_tensor)])

    def spread(own, quarter, core):
        rows = own.shape[0]
        half = rows // 16 * 8
        from_x = flip_x(own)
        from_y = flip_y(own)
        diag = jnp.concatenate([flip_x(from_y[:half]), flip_y(from_x[half:])])
        four = jnp.stack([own, from_x, from_y, diag])
        other = flip_core(four)
        four = jnp.stack([four[quarter ^ j] for j in range(4)])
        other = jnp.stack([other[quarter ^ j] for j in range(4)])
        return jnp.where(core == 0, jnp.concatenate([four, other]), jnp.concatenate([other, four]))

    def gather_rows(values, index):
        pieces = [values]
        for _ in range(n_tensor - 1):
            pieces.append(ring(pieces[-1]))
        rows = values.shape[0]
        out = jnp.zeros((n_tensor * rows, values.shape[1]), values.dtype)
        for step, piece in enumerate(pieces):
            out = lax.dynamic_update_slice(out, piece, (((index - step) % n_tensor) * rows, 0))
        return out

    def shards(
        hidden_in, query_weight, query_bias, key_weight, value_weight, value_bias,
        output_weight, output_bias, attn_gain, attn_shift, up_weight, up_bias,
        down_weight, down_bias, ffn_gain, ffn_shift, cotangent,
    ):
        width = hidden_in.shape[1]
        rows = hidden_in.shape[0] // n_tensor
        seqs = rows // LEN
        head_block = query_weight.shape[1]
        ff_block = up_weight.shape[1]
        heads = head_block // HDIM
        score_scale = HDIM ** (-0.5)
        t = lax.axis_index("tensor")
        r = lax.axis_index("dp") % GROUP
        core = r & 1
        quarter = r >> 1
        position = core * 4 + quarter

        x = lax.dynamic_slice(hidden_in, (t * rows, 0), (rows, width))
        cot = lax.dynamic_slice(cotangent, (t * rows, 0), (rows, width))
        slice_rows = 4 * head_block // GROUP
        ff_slice = ff_block // GROUP

        pack_attn = jnp.concatenate([query_weight.T, key_weight.T, value_weight.T, output_weight])
        pack_up = up_weight.T
        pack_down = down_weight

        def take(pack, size):
            return lax.dynamic_slice(pack, (position * size, 0), (size, width))

        bias_rows = jnp.zeros((8, width), bf16)
        bias_rows = bias_rows.at[0, :ff_block].set(up_bias)
        bias_rows = bias_rows.at[1, :head_block].set(query_bias)
        bias_rows = bias_rows.at[2, :head_block].set(value_bias)

        def gather_pack(pack, size, extra=None):
            own = take(pack, size)
            sent = own if extra is None else jnp.concatenate([own, extra])
            got = [flip_tensor(sent, k) for k in range(1, n_tensor)]
            z = jnp.concatenate([g[:size] for g in got])
            full = spread(z, quarter, core)
            full = full.reshape(GROUP, n_tensor - 1, size, width).transpose(1, 0, 2, 3)
            full = full.reshape(n_tensor - 1, GROUP * size, width)
            full = jnp.concatenate([pack[None], full])
            return full, [g[size:] for g in got]

        attn_all, extras = gather_pack(pack_attn, slice_rows, bias_rows)
        up_all, _ = gather_pack(pack_up, ff_slice)
        down_all, _ = gather_pack(pack_down, ff_slice)
        biases = jnp.stack([bias_rows] + extras)
        wq, wk, wv, wo = [
            attn_all[:, i * head_block : (i + 1) * head_block].reshape(n_tensor * head_block, width)
            for i in range(4)
        ]
        wu = up_all.reshape(n_tensor * ff_block, width)
        wd = down_all.reshape(n_tensor * ff_block, width)
        up_b = biases[:, 0, :ff_block].reshape(-1).astype(f32)
        query_b = biases[:, 1, :head_block].reshape(-1).astype(f32)
        value_b = biases[:, 2, :head_block].reshape(-1).astype(f32)

        nt = ((1,), (1,))
        nn = ((1,), (0,))
        tn = ((0,), (0,))
        all_heads = n_tensor * heads
        head_shape = (seqs, LEN, all_heads, HDIM)
        inputs = x.astype(f32)
        queries = (dot(x, wq, nt) + query_b).astype(bf16)
        keys = dot(x, wk, nt).astype(bf16)
        values = (dot(x, wv, nt) + value_b).astype(bf16)
        qh, kh, vh = (v.reshape(head_shape) for v in (queries, keys, values))
        scores = jnp.einsum("bqhd,bkhd->bhqk", qh, kh, preferred_element_type=f32) * score_scale
        peak = jnp.max(scores, axis=-1, keepdims=True)
        exp_scores = jnp.exp(scores - peak)
        total = jnp.sum(exp_scores, axis=-1, keepdims=True)
        probs = (exp_scores / total).astype(bf16)
        log_total = peak + jnp.log(total)
        mixed = jnp.einsum("bhqk,bkhd->bqhd", probs, vh, preferred_element_type=f32)
        mixed = mixed.reshape(rows, n_tensor * head_block).astype(bf16)
        attn = dot(mixed, wo, nn)
        hat1, inv1 = norm_parts(inputs + attn + output_bias.astype(f32))
        first = hat1 * attn_gain.astype(f32) + attn_shift.astype(f32)
        first_low = first.astype(bf16)
        pre = dot(first_low, wu, nt) + up_b
        active = jax.nn.gelu(pre, approximate=False).astype(bf16)
        ffn = dot(active, wd, nn)
        hat2, inv2 = norm_parts(first + ffn + down_bias.astype(f32))
        out_rows = (hat2 * ffn_gain.astype(f32) + ffn_shift.astype(f32)).astype(bf16)
        layer_out = gather_rows(out_rows, t)

        grad_out = cot.astype(f32)
        sums = {}
        sums["ffn_gain"] = jnp.sum(grad_out * hat2, axis=0)
        sums["ffn_shift"] = jnp.sum(grad_out, axis=0)
        grad_second = norm_back(grad_out, hat2, inv2, ffn_gain)
        sums["down_bias"] = jnp.sum(grad_second, axis=0)
        second_low = grad_second.astype(bf16)
        grad_pre = (dot(second_low, wd, nt) * gelu_slope(pre)).astype(bf16)
        sums["up_bias"] = jnp.sum(grad_pre, axis=0, dtype=f32)
        grad_first = grad_second + dot(grad_pre, wu, nn)
        sums["attn_gain"] = jnp.sum(grad_first * hat1, axis=0)
        sums["attn_shift"] = jnp.sum(grad_first, axis=0)
        grad_resid = norm_back(grad_first, hat1, inv1, attn_gain)
        sums["output_bias"] = jnp.sum(grad_resid, axis=0)
        resid_low = grad_resid.astype(bf16)
        grad_context = dot(resid_low, wo, nt).astype(bf16).reshape(head_shape)
        scores_again = jnp.einsum("bqhd,bkhd->bhqk", qh, kh, preferred_element_type=f32) * score_scale
        probs_full = jnp.exp(scores_again - log_total)
        probs_low = probs_full.astype(bf16)
        value_grad = jnp.einsum("bhqk,bqhd->bkhd", probs_low, grad_context, preferred_element_type=f32)
        value_grad = value_grad.reshape(rows, -1).astype(bf16)
        grad_probs = jnp.einsum("bqhd,bkhd->bhqk", grad_context, vh, preferred_element_type=f32)
        inner = jnp.sum(probs_full * grad_probs, axis=-1, keepdims=True)
        grad_scores = (probs_full * (grad_probs - inner)).astype(bf16)
        query_grad = jnp.einsum("bhqk,bkhd->bqhd", grad_scores, kh, preferred_element_type=f32)
        query_grad = (query_grad * score_scale).reshape(rows, -1).astype(bf16)
        key_grad = jnp.einsum("bhqk,bqhd->bkhd", grad_scores, qh, preferred_element_type=f32)
        key_grad = (key_grad * score_scale).reshape(rows, -1).astype(bf16)
        sums["query_bias"] = jnp.sum(query_grad, axis=0, dtype=f32)
        sums["value_bias"] = jnp.sum(value_grad, axis=0, dtype=f32)
        input_rows = (
            grad_resid + dot(query_grad, wq, nn) + dot(key_grad, wk, nn) + dot(value_grad, wv, nn)
        ).astype(bf16)
        input_grad = gather_rows(input_rows, t)

        def half(left, block):
            v = left.reshape(rows, n_tensor, 2, block // 2)
            mine = lax.dynamic_index_in_dim(v, core, 2, keepdims=False).reshape(rows, -1)
            sent = lax.dynamic_index_in_dim(v, 1 - core, 2, keepdims=False).reshape(rows, -1)
            return jnp.concatenate([mine, flip_core(sent)])

        def both(right):
            return jnp.concatenate([right, flip_core(right)])

        def scatter(grad, size):
            g = grad.astype(bf16).reshape(n_tensor, 2, 2, size, width)
            xb, yb = quarter & 1, quarter >> 1
            lo, hi = g[: n_tensor // 2], g[n_tensor // 2 :]

            def pick(v, axis, index):
                return lax.dynamic_index_in_dim(v, index, axis, keepdims=False)

            lo = pick(lo, 2, xb).astype(f32) + flip_x(pick(lo, 2, 1 - xb)).astype(f32)
            hi = pick(hi, 1, yb).astype(f32) + flip_y(pick(hi, 1, 1 - yb)).astype(f32)
            lo = lo.astype(bf16)
            hi = hi.astype(bf16)
            lo = pick(lo, 1, yb).astype(f32) + flip_y(pick(lo, 1, 1 - yb)).astype(f32)
            hi = pick(hi, 1, xb).astype(f32) + flip_x(pick(hi, 1, 1 - xb)).astype(f32)
            mine = jnp.concatenate([lo, hi])
            low = mine.astype(bf16)
            total = mine[0]
            for k in range(1, n_tensor):
                total = total + flip_tensor(low[k], k).astype(f32)
            return total

        def weight_grad(left, right, block):
            return dot(half(left, block), both(right), tn).reshape(n_tensor, block // 2, width)

        down_slice = scatter(weight_grad(active, second_low, ff_block), ff_slice)
        up_slice = scatter(weight_grad(grad_pre, first_low, ff_block), ff_slice)
        attn_left = jnp.stack(
            [v.reshape(rows, n_tensor, head_block) for v in (query_grad, key_grad, value_grad, mixed)], axis=2
        )
        first_half = attn_left[:, :, :2].reshape(rows, -1)
        last_half = attn_left[:, :, 2:].reshape(rows, -1)
        mine = jnp.where(core == 0, first_half, last_half)
        sent = jnp.where(core == 0, last_half, first_half)
        left = jnp.concatenate([mine, flip_core(sent)])
        xs = both(x)
        rs = both(resid_low)
        left = left.reshape(2 * rows, n_tensor, 2, head_block)
        p0 = dot(left[:, :, 0].reshape(2 * rows, -1), xs, tn).reshape(n_tensor, head_block, width)
        right = jnp.where(core == 0, xs, rs)
        p1 = dot(left[:, :, 1].reshape(2 * rows, -1), right, tn).reshape(n_tensor, head_block, width)
        attn_slice = scatter(jnp.concatenate([p0, p1], axis=1), slice_rows)
        slices = jnp.concatenate([down_slice, up_slice, attn_slice])

        def blocks(values, block):
            v = values.reshape(n_tensor, block)
            v = jnp.where((t & 1) == 1, v.reshape(n_tensor // 2, 2, block)[:, ::-1].reshape(v.shape), v)
            return jnp.where((t & 2) == 2, jnp.concatenate([v[2:], v[:2]]), v)

        small = jnp.concatenate([
            blocks(sums["up_bias"], ff_block).reshape(-1),
            blocks(sums["query_bias"], head_block).reshape(-1),
            blocks(sums["value_bias"], head_block).reshape(-1),
            sums["output_bias"], sums["attn_gain"], sums["attn_shift"],
            sums["down_bias"], sums["ffn_gain"], sums["ffn_shift"],
        ])
        small = small.reshape(-1, width)
        for bit in (1, 2, 4):
            small = small + flip_dp(small, bit)
        for bit in (1, 2):
            small = small + flip_tensor(small, bit)
        if n_dp > GROUP:
            groups = [[g * GROUP + i for g in range(n_dp // GROUP)] for i in range(GROUP)]
            slices = lax.psum(slices, "dp", axis_index_groups=groups)
            small = lax.psum(small, "dp", axis_index_groups=groups)
        full = spread(slices.astype(bf16), quarter, core).astype(f32)
        down_grad = full[:, :ff_slice].reshape(ff_block, width)
        up_grad = full[:, ff_slice : 2 * ff_slice].reshape(ff_block, width).T
        attn_grad = full[:, 2 * ff_slice :].reshape(4 * head_block, width)
        small = small.reshape(-1)
        pos = [0]

        def part(count):
            v = small[pos[0] : pos[0] + count]
            pos[0] += count
            return v

        def own(count, block):
            v = part(count).reshape(n_tensor, block)
            return lax.dynamic_index_in_dim(v, t, 0, keepdims=False)

        up_bias_grad = own(n_tensor * ff_block, ff_block)
        query_bias_grad = own(n_tensor * head_block, head_block)
        value_bias_grad = own(n_tensor * head_block, head_block)
        (output_bias_grad, attn_gain_grad, attn_shift_grad, down_bias_grad, ffn_gain_grad, ffn_shift_grad) = [
            part(width) for _ in range(6)
        ]
        return (
            layer_out, input_grad,
            attn_grad[:head_block].T, query_bias_grad,
            attn_grad[head_block : 2 * head_block].T,
            attn_grad[2 * head_block : 3 * head_block].T, value_bias_grad,
            attn_grad[3 * head_block :], output_bias_grad, attn_gain_grad, attn_shift_grad,
            up_grad, up_bias_grad, down_grad, down_bias_grad, ffn_gain_grad, ffn_shift_grad,
        )

    return shards


def solution(mesh):
    in_specs = (
        P("dp", None), P(None, "tensor"), P("tensor"), P(None, "tensor"), P(None, "tensor"), P("tensor"),
        P("tensor", None), P(), P(), P(), P(None, "tensor"), P("tensor"), P("tensor", None), P(), P(), P(),
        P("dp", None),
    )
    out_specs = (
        P("dp", None), P("dp", None), P(None, "tensor"), P("tensor"), P(None, "tensor"), P(None, "tensor"),
        P("tensor"), P("tensor", None), P(), P(), P(), P(None, "tensor"), P("tensor"), P("tensor", None),
        P(), P(), P(),
    )
    shards = make_shards(mesh.shape["dp"], mesh.shape["tensor"])
    return jax.shard_map(shards, mesh=mesh, in_specs=in_specs, out_specs=out_specs, check_vma=False)
```
